128 devices in a mesh: tm: 4 (over x), panel: 32 (over y, z, core).
Axes of the slice: x: 4, y: 4, z: 4, core: 2. Of those that a mesh axis runs over, the one named last changes fastest.
Arguments:
- separator_cov: float32 [4, 2048, 2048], P('tm', 'panel'), may hold values from -6 to 6
- separator_arrow: float32 [4, 6, 2048], P('tm'), may hold values from -6 to 6
- coupling: float32 [4, 2048, 2048], P('tm', 'panel'), may hold values from -0.25 to 0.25
- arrow_factor: float32 [4, 6, 2048], P('tm'), may hold values from -6 to 6
- arrow_tip: float32 [6, 6], replicated, may hold values from -6 to 6
- inverse_gram: float32 [4, 2048, 2048], P('tm', 'panel'), may hold values from -6 to 6
Outputs:
- diag_cov: float32 [4, 2048, 2048], P('tm', 'panel')
- off_diag: float32 [4, 2048, 2048], P('tm', 'panel')
- arrow_cov: float32 [4, 6, 2048], P('tm', None, 'panel')
The draws below stay inside these ranges and needn't reach their ends.
All inputs are finite; a program needn't handle non-finite values.
Results may differ from the reference program's by a relative error of at most 0.0001.
Values sent between devices are 32-bit elements; how exact they have to be, the bound alone decides.
No kernel may reach another device: no remote copies, remote signals or barrier semaphores. Data moves between devices by JAX's collectives and lax.ppermute only.
A program may use at most 128 MiB of HBM per device.

```python
import jax
import jax.numpy as jnp
from jax import lax

NODES = 2048
ARROW = 6
PARTS_SIZE = 4
N_TM = 4


def with_spikes(entries, own_key, source, target, shards_of, factor):
    def block_of(dim):
        return (jnp.arange(entries.shape[dim]) // (entries.shape[dim] // shards_of)).reshape((-1,) + (1,) * (entries.ndim - 1 - dim))

    near = jax.random.permutation(own_key, shards_of)[block_of(target)]
    other_side = (block_of(target) + shards_of // 2) % shards_of
    return jnp.where((block_of(source) == near) | (block_of(source) == other_side), factor * entries, entries)


def levels(own_key, shape, shards, least, top_value):
    level, own = 1.0, jax.random.fold_in(own_key, 6)
    for axis_at, parts in shards:
        steps = jnp.exp(jax.random.uniform(jax.random.fold_in(own, axis_at), (parts,), jnp.float32, least / len(shards), top_value / len(shards)))
        level = level * jnp.repeat(steps, shape[axis_at] // parts).reshape([-1 if axis == axis_at else 1 for axis in range(len(shape))])
    return level


def scatter_about(rng, dims, deviation, reach, pieces=(), kind=jnp.bfloat16):
    level = levels(rng, dims, pieces, -0.22, 0.18) if pieces else 1.0
    result = jax.random.normal(rng, dims, jnp.float32) * deviation * level
    return jnp.minimum(jnp.maximum(result, -reach), reach).astype(kind)


def gaussian_with(rng, dims, spread, limit, cuts, heavy, held_as=jnp.bfloat16):
    result = spread * jax.random.normal(rng, dims, jnp.float32)
    if cuts:
        result = result * levels(rng, dims, cuts, -0.22, 0.18)
    return jnp.clip(with_spikes(result, jax.random.fold_in(rng, 3), *heavy), -limit, limit).astype(held_as)


def setup_inputs(seed: int = 0) -> dict:
    key_of = jax.random.split(jax.random.key(seed), 7)
    separator_cov = scatter_about(key_of[0], (PARTS_SIZE, NODES, NODES), 1.0, 6.0, ((0, 4), (1, 32)), jnp.float32)
    separator_arrow = scatter_about(key_of[1], (PARTS_SIZE, ARROW, NODES), 1.0, 6.0, ((0, 4),), jnp.float32)
    coupling = gaussian_with(key_of[2], (PARTS_SIZE, NODES, NODES), NODES ** -0.5, 0.25, ((0, 4), (1, 32)), (1, 2, 32, 2.75), jnp.float32)
    arrow_factor = scatter_about(key_of[3], (PARTS_SIZE, ARROW, NODES), 1.0, 6.0, ((0, 4),), jnp.float32)
    arrow_tip = scatter_about(key_of[4], (ARROW, ARROW), 0.4, 6.0, (), jnp.float32)
    inverse_gram = scatter_about(key_of[5], (PARTS_SIZE, NODES, NODES), 1.0, 6.0, ((0, 4), (1, 32)), jnp.float32)
    return {"separator_cov": separator_cov, "separator_arrow": separator_arrow, "coupling": coupling, "arrow_factor": arrow_factor, "arrow_tip": arrow_tip, "inverse_gram": inverse_gram}


def matmul(left, right):
    return jnp.dot(left, right, preferred_element_type=jnp.float32, precision=lax.Precision.HIGHEST)


def reference(separator_cov, separator_arrow, coupling, arrow_factor, arrow_tip, inverse_gram):
    diag_list = []
    lower_list = []
    arrow_list = []
    for part in range(N_TM):
        if part + 1 < N_TM:
            next_cov = separator_cov[part + 1]
            next_arrow = separator_arrow[part + 1]
        else:
            next_cov = jnp.zeros_like(separator_cov[0])
            next_arrow = jnp.zeros_like(separator_arrow[0])
        factor = coupling[part]
        arrow_rows = arrow_factor[part]
        lower = -(matmul(next_cov, factor) + matmul(next_arrow.T, arrow_rows))
        arrow_out = -(matmul(next_arrow, factor) + matmul(arrow_tip, arrow_rows))
        diag_out = inverse_gram[part] - matmul(factor.T, lower) - matmul(arrow_rows.T, arrow_out)
        diag_list.append(diag_out)
        lower_list.append(lower)
        arrow_list.append(arrow_out)
    return jnp.stack(diag_list), jnp.stack(lower_list), jnp.stack(arrow_list)
```

```python
import functools

import jax
import jax.numpy as jnp
from jax import lax
from jax.experimental import pallas as pl
from jax.experimental.pallas import tpu as pltpu
from jax.sharding import PartitionSpec as P

SIDE = 4
CHUNKS = 2


def panel_index(y, z, core):
    return (y % SIDE) * 2 * SIDE + (z % SIDE) * 2 + core


def route(target):
    places = [(y, z, core) for y in range(SIDE) for z in range(SIDE) for core in range(2)]
    return [(panel_index(*place), panel_index(*target(*place))) for place in places]


def along_y(block, distance):
    return lax.ppermute(block, "panel", route(lambda y, z, core: (y + distance, z, core)))


def along_z(block, distance):
    return lax.ppermute(block, "panel", route(lambda y, z, core: (y, z + distance, core)))


def to_other_core(block):
    return lax.ppermute(block, "panel", route(lambda y, z, core: (y, z, 1 - core)))


def to_previous_step(block, distance):
    size = 2 * SIDE * SIDE
    steps = range(1, lax.axis_size("tm"))
    pairs = [
        (step * size + source, (step - 1) * size + target)
        for step in steps
        for source, target in route(lambda y, z, core: (y + distance, z, core))
    ]
    return lax.ppermute(block, ("tm", "panel"), pairs)


def position():
    index = lax.axis_index("panel")
    return index // (2 * SIDE), (index // 2) % SIDE, index % 2


def ds(index, size):
    return pl.ds(pl.multiple_of(index * size, size), size)


def split(value):
    high = value.astype(jnp.bfloat16)
    return high, (value - high.astype(jnp.float32)).astype(jnp.bfloat16)


def dot(left, right):
    return jnp.dot(left, right, preferred_element_type=jnp.float32)


def dot_rows(left, right):
    return lax.dot_general(
        left, right, (((0,), (0,)), ((), ())), preferred_element_type=jnp.float32, precision=lax.Precision.HIGHEST
    )


def call(kernel, out_shape, *operands, name):
    spec = pl.BlockSpec(memory_space=pltpu.VMEM)
    return pl.pallas_call(
        kernel,
        out_shape=out_shape,
        in_specs=[spec] * len(operands),
        out_specs=jax.tree.map(lambda _: spec, out_shape),
        name=name,
    )(*operands)


def f32(*shape):
    return jax.ShapeDtypeStruct(shape, jnp.float32)


def bf16(*shape):
    return jax.ShapeDtypeStruct(shape, jnp.bfloat16)


def cut_separator(cov_ref, arrow_ref, *out_refs):
    y, _, _ = position()
    for distance, out in enumerate(out_refs):
        strip = ds(lax.rem(y + SIDE - distance, SIDE), 512)
        out[:64, :] = cov_ref[:, strip]
        if distance == 0:
            out[64:, :] = jnp.zeros_like(out[64:, :])
            out[64:70, :] = arrow_ref[:, strip]


def pair_rows(own_ref, other_ref, *out_refs):
    _, _, core = position()
    width = out_refs[0].shape[1]
    for chunk, out in enumerate(out_refs):
        columns = pl.ds(pl.multiple_of(core * 1024 + chunk * width, 128), width)
        out[ds(core, 64), :] = own_ref[:, columns]
        out[ds(1 - core, 64), :] = other_ref[:, columns]


def lay_separator(*refs):
    own, other, (high_ref, low_ref, arrow_ref) = refs[:4], refs[4:8], refs[8:]
    _, z, core = position()
    for block in range(SIDE):
        columns = ds(lax.rem(z + block, SIDE), 128)
        to = slice(128 * block, 128 * block + 128)
        for distance in range(SIDE):
            for where, source in ((core, own), (1 - core, other)):
                rows = pl.ds(pl.multiple_of(128 * distance + 64 * where, 64), 64)
                high, low = split(source[distance][:64, columns])
                high_ref[rows, to] = high
                low_ref[rows, to] = low
        high, low = split(own[0][64:, columns])
        pad = jnp.zeros((8, 128), jnp.float32)
        high_ref[512:, to] = jnp.concatenate([high.astype(jnp.float32), pad]).astype(jnp.bfloat16)
        low_ref[512:, to] = jnp.concatenate([low.astype(jnp.float32), pad]).astype(jnp.bfloat16)
        if block == 0:
            arrow_ref[...] = own[0][64:, columns]


def multiply(*refs):
    (high_ref, low_ref), pieces, outs = refs[:2], refs[2:6], refs[6:]
    high, low = split(jnp.concatenate([piece[...] for piece in pieces]))
    left_high, left_low = high_ref[...], low_ref[...]
    product = dot(left_high, high) + (dot(left_high, low) + dot(left_low, high))
    for distance, out in enumerate(outs):
        out[:128, :] = product[128 * distance : 128 * distance + 128]
        if out.shape[0] > 128:
            out[128:, :] = product[512:520]


def fold_lower(chunk, parts, arrow_ref, factor_ref, tip_ref, lower_ref, sent_ref, tail_ref):
    _, _, core = position()
    width = lower_ref.shape[1]
    columns = pl.ds(pl.multiple_of(core * 1024 + chunk * width, 128), width)
    total = (parts[0][...] + parts[1][...]) + (parts[2][...] + parts[3][...])
    factor = factor_ref[:, columns]
    lower_ref[...] = total[:128] + dot_rows(arrow_ref[:6, :], factor)
    sent_ref[...] = lower_ref[ds(1 - core, 64), :]
    tail_ref[...] = jnp.zeros_like(tail_ref)
    tail_ref[:6, :] = total[128:134] + jnp.dot(
        tip_ref[...], factor, preferred_element_type=jnp.float32, precision=lax.Precision.HIGHEST
    )


def fold_kernel(chunk, *refs):
    fold_lower(chunk, refs[:4], *refs[4:])


def pick_columns(*refs):
    pieces, out = refs[:-1], refs[-1]
    _, z, _ = position()
    chunks = len(pieces) // SIDE
    blocks = 8 // chunks
    for piece in range(SIDE):
        rows = slice(128 * piece, 128 * piece + 128)
        for half in range(2):
            first = half * SIDE
            if blocks >= SIDE:
                source = pieces[(first // blocks) * SIDE + piece]
                value = source[:, ds(first % blocks + z, 128)]
            else:
                low = pieces[(first // blocks) * SIDE + piece][:, ds(lax.rem(z, blocks), 128)]
                high = pieces[(first // blocks + 1) * SIDE + piece][:, ds(lax.rem(z, blocks), 128)]
                value = jnp.where(z < blocks, low, high)
            out[rows, 128 * half : 128 * half + 128] = value


def turn_columns(own_ref, other_ref, high_ref, low_ref, all_ref):
    y, _, core = position()
    for half in range(2):
        columns = slice(128 * half, 128 * half + 128)
        all_ref[2 * core + half] = own_ref[:, columns].T
        all_ref[2 * (1 - core) + half] = other_ref[:, columns].T
    for distance in range(SIDE):
        rows = slice(128 * distance, 128 * distance + 128)
        high, low = split(all_ref[lax.rem(y + distance, SIDE)])
        high_ref[rows, :] = high
        low_ref[rows, :] = low


def sum_diagonal(*refs):
    parts, (factor_ref, tail_ref, kept_ref, sent_ref, all_ref) = refs[:4], refs[4:]
    y, z, core = position()
    factor = factor_ref[:, ds(y * SIDE + z, 128)]
    total = (parts[0][...] + parts[1][...]) + (parts[2][...] + parts[3][...])
    all_ref[...] = total + dot_rows(factor, tail_ref[:6, :])
    kept_ref[...] = all_ref[ds(core, 64), :]
    sent_ref[...] = all_ref[ds(1 - core, 64), :]


def finish_lower(chunks, *refs):
    lowers, others = refs[:chunks], refs[chunks : 2 * chunks]
    tails, other_tails = refs[2 * chunks : 3 * chunks], refs[3 * chunks : 4 * chunks]
    lower_ref, arrow_ref, tail_ref = refs[4 * chunks :]
    y, z, core = position()
    width = lowers[0].shape[1]
    for chunk in range(chunks):
        own = pl.ds(pl.multiple_of(core * 1024 + chunk * width, 128), width)
        other = pl.ds(pl.multiple_of((1 - core) * 1024 + chunk * width, 128), width)
        lower_ref[0, :, own] = -lowers[chunk][ds(core, 64), :]
        lower_ref[0, :, other] = -others[chunk][...]
        tail_ref[:, own] = tails[chunk][...]
        tail_ref[:, other] = other_tails[chunk][...]
    block = tail_ref[:, ds(y * SIDE + z, 128)]
    share = jnp.where(core == 0, block[:, :64], block[:, 64:])
    arrow_ref[0] = -share[:6]


def finish_diagonal(chunks, *refs):
    gram_ref, own_refs, other_refs, out_ref = refs[0], refs[1 : 1 + chunks], refs[1 + chunks : 1 + 2 * chunks], refs[-1]
    _, _, core = position()
    width = own_refs[0].shape[1]
    for chunk in range(chunks):
        own = pl.ds(pl.multiple_of(core * 1024 + chunk * width, 128), width)
        other = pl.ds(pl.multiple_of((1 - core) * 1024 + chunk * width, 128), width)
        out_ref[0, :, own] = gram_ref[0, :, own] + own_refs[chunk][...]
        out_ref[0, :, other] = gram_ref[0, :, other] + other_refs[chunk][...]


def per_device(separator_cov, separator_arrow, coupling, arrow_factor, arrow_tip, inverse_gram):
    width = 1024 // CHUNKS
    factor = arrow_factor[0]

    strips = call(
        cut_separator, [f32(72, 512)] + [f32(64, 512)] * 3, separator_cov[0], separator_arrow[0], name="cut_separator"
    )
    own_strips = [to_previous_step(strip, -distance) for distance, strip in enumerate(strips)]
    rows = coupling[0]
    starts = call(pair_rows, [f32(128, width)] * CHUNKS, rows, to_other_core(rows), name="pair_rows")

    def gathered(block):
        return [block] + [along_z(block, -distance) for distance in (1, 2, 3)]

    pieces = [gathered(start) for start in starts]
    other_strips = [to_other_core(strip[:64]) for strip in own_strips]
    high, low, arrow = call(
        lay_separator, [bf16(528, 512), bf16(528, 512), f32(8, 128)], *own_strips, *other_strips, name="lay_separator"
    )

    lowers, sents, tails = [], [], []
    for chunk in range(CHUNKS):
        shares = call(multiply, [f32(136, width)] * SIDE, high, low, *pieces[chunk], name="multiply")
        parts = [shares[0]] + [along_y(shares[distance], distance) for distance in (1, 2, 3)]
        lower, sent, tail = call(
            functools.partial(fold_kernel, chunk),
            [f32(128, width), f32(64, width), f32(8, width)],
            *parts,
            arrow,
            factor,
            arrow_tip,
            name="fold_lower",
        )
        lowers.append(lower)
        sents.append(sent)
        tails.append(tail)

    columns = call(pick_columns, f32(512, 256), *[piece for chunk in pieces for piece in chunk], name="pick_columns")
    turned = pl.pallas_call(
        turn_columns,
        out_shape=[bf16(512, 512)] * 2,
        in_specs=[pl.BlockSpec(memory_space=pltpu.VMEM)] * 2,
        out_specs=[pl.BlockSpec(memory_space=pltpu.VMEM)] * 2,
        scratch_shapes=[pltpu.VMEM((SIDE, 128, 512), jnp.float32)],
        name="turn_columns",
    )(columns, to_other_core(columns))

    kept, others = [], []
    for chunk in range(CHUNKS):
        shares = call(multiply, [f32(128, width)] * SIDE, *turned, *gathered(lowers[chunk]), name="multiply")
        parts = [shares[0]] + [along_y(shares[distance], distance) for distance in (1, 2, 3)]
        mine, sent = pl.pallas_call(
            sum_diagonal,
            out_shape=[f32(64, width)] * 2,
            in_specs=[pl.BlockSpec(memory_space=pltpu.VMEM)] * 6,
            out_specs=[pl.BlockSpec(memory_space=pltpu.VMEM)] * 2,
            scratch_shapes=[pltpu.VMEM((128, width), jnp.float32)],
            name="sum_diagonal",
        )(*parts, factor, tails[chunk])
        kept.append(mine)
        others.append(to_other_core(sent))

    lower_out, arrow_out = pl.pallas_call(
        functools.partial(finish_lower, CHUNKS),
        out_shape=[f32(1, 64, 2048), f32(1, 6, 64)],
        in_specs=[pl.BlockSpec(memory_space=pltpu.VMEM)] * (4 * CHUNKS),
        out_specs=[pl.BlockSpec(memory_space=pltpu.VMEM)] * 2,
        scratch_shapes=[pltpu.VMEM((8, 2048), jnp.float32)],
        name="finish_lower",
    )(*lowers, *[to_other_core(sent) for sent in sents], *tails, *[to_other_core(tail) for tail in tails])
    diag_out = call(
        functools.partial(finish_diagonal, CHUNKS), f32(1, 64, 2048), inverse_gram, *kept, *others, name="finish_diagonal"
    )
    return diag_out, lower_out, arrow_out


def solution(mesh):
    return jax.shard_map(
        per_device,
        mesh=mesh,
        in_specs=(
            P("tm", "panel", None),
            P("tm", None, None),
            P("tm", "panel", None),
            P("tm", None, None),
            P(),
            P("tm", "panel", None),
        ),
        out_specs=(P("tm", "panel", None), P("tm", "panel", None), P("tm", None, "panel")),
        check_vma=False,
    )
```

```python
import functools

import jax
import jax.numpy as jnp
from jax import lax
from jax.experimental import pallas as pl
from jax.experimental.pallas import tpu as pltpu
from jax.sharding import PartitionSpec as P

SIDE = 4
CHUNKS = 2
GRANT = 12 * 2**20


def panel_index(y, z, core):
    return (y % SIDE) * 2 * SIDE + (z % SIDE) * 2 + core


def route(target):
    places = [(y, z, core) for y in range(SIDE) for z in range(SIDE) for core in range(2)]
    return [(panel_index(*place), panel_index(*target(*place))) for place in places]


def along_y(block, distance):
    return lax.ppermute(block, "panel", route(lambda y, z, core: (y + distance, z, core)))


def along_z(block, distance):
    return lax.ppermute(block, "panel", route(lambda y, z, core: (y, z + distance, core)))


def to_other_core(block):
    return lax.ppermute(block, "panel", route(lambda y, z, core: (y, z, 1 - core)))


def to_previous_step(block, distance):
    size = 2 * SIDE * SIDE
    steps = range(1, lax.axis_size("tm"))
    pairs = [
        (step * size + source, (step - 1) * size + target)
        for step in steps
        for source, target in route(lambda y, z, core: (y + distance, z, core))
    ]
    return lax.ppermute(block, ("tm", "panel"), pairs)


def position():
    index = lax.axis_index("panel")
    return index // (2 * SIDE), (index // 2) % SIDE, index % 2


def ds(index, size):
    return pl.ds(pl.multiple_of(index * size, size), size)


def split(value):
    high = value.astype(jnp.bfloat16)
    return high, (value - high.astype(jnp.float32)).astype(jnp.bfloat16)


def dot(left, right):
    return jnp.dot(left, right, preferred_element_type=jnp.float32)


def dot_rows(left, right):
    return lax.dot_general(
        left, right, (((0,), (0,)), ((), ())), preferred_element_type=jnp.float32, precision=lax.Precision.HIGHEST
    )


def call(kernel, out_shape, *operands, name, scratch=()):
    spec = pl.BlockSpec(memory_space=pltpu.VMEM)
    return pl.pallas_call(
        kernel,
        out_shape=out_shape,
        in_specs=[spec] * len(operands),
        out_specs=jax.tree.map(lambda _: spec, out_shape),
        scratch_shapes=scratch,
        compiler_params=pltpu.CompilerParams(vmem_limit_bytes=GRANT),
        name=name,
    )(*[pltpu.with_memory_space_constraint(operand, pltpu.VMEM) for operand in operands])


def f32(*shape):
    return pltpu.VMEM(shape, jnp.float32)


def bf16(*shape):
    return pltpu.VMEM(shape, jnp.bfloat16)


def given(*shape):
    return jax.ShapeDtypeStruct(shape, jnp.float32)


def cut_separator(cov_ref, arrow_ref, *out_refs):
    y, _, _ = position()
    for distance, out in enumerate(out_refs):
        strip = ds(lax.rem(y + SIDE - distance, SIDE), 512)
        out[:64, :] = cov_ref[:, strip]
        if distance == 0:
            out[64:, :] = jnp.zeros_like(out[64:, :])
            for row in range(6):
                out[64 + row : 65 + row, :] = arrow_ref[row, :, strip]


def pair_rows(own_ref, other_ref, *out_refs):
    _, _, core = position()
    width = out_refs[0].shape[1]
    for chunk, out in enumerate(out_refs):
        columns = pl.ds(pl.multiple_of(core * 1024 + chunk * width, 128), width)
        out[ds(core, 64), :] = own_ref[:, columns]
        out[ds(1 - core, 64), :] = other_ref[:, columns]


def lay_separator(*refs):
    own, other, (high_ref, low_ref, arrow_ref) = refs[:4], refs[4:8], refs[8:]
    _, z, core = position()
    for block in range(SIDE):
        columns = ds(lax.rem(z + block, SIDE), 128)
        to = slice(128 * block, 128 * block + 128)
        for distance in range(SIDE):
            for where, source in ((core, own), (1 - core, other)):
                rows = pl.ds(pl.multiple_of(128 * distance + 64 * where, 64), 64)
                high, low = split(source[distance][:64, columns])
                high_ref[rows, to] = high
                low_ref[rows, to] = low
        high, low = split(own[0][64:, columns])
        pad = jnp.zeros((8, 128), jnp.float32)
        high_ref[512:, to] = jnp.concatenate([high.astype(jnp.float32), pad]).astype(jnp.bfloat16)
        low_ref[512:, to] = jnp.concatenate([low.astype(jnp.float32), pad]).astype(jnp.bfloat16)
        if block == 0:
            arrow_ref[...] = own[0][64:, columns]


def multiply(*refs):
    (high_ref, low_ref), pieces, outs = refs[:2], refs[2:6], refs[6:]
    high, low = split(jnp.concatenate([piece[...] for piece in pieces]))
    left_high, left_low = high_ref[...], low_ref[...]
    product = dot(left_high, high) + (dot(left_high, low) + dot(left_low, high))
    for distance, out in enumerate(outs):
        out[:128, :] = product[128 * distance : 128 * distance + 128]
        if out.shape[0] > 128:
            out[128:, :] = product[512:520]


def factor_rows(factor_ref, rows_ref, columns):
    for row in range(6):
        rows_ref[row : row + 1, :] = factor_ref[row, :, columns]
    return rows_ref[:6, :]


def fold_lower(chunk, *refs):
    parts, (arrow_ref, factor_ref, tip_ref, lower_ref, sent_ref, tail_ref, rows_ref) = refs[:4], refs[4:]
    _, _, core = position()
    width = lower_ref.shape[1]
    factor = factor_rows(factor_ref, rows_ref, pl.ds(pl.multiple_of(core * 1024 + chunk * width, 128), width))
    total = (parts[0][...] + parts[1][...]) + (parts[2][...] + parts[3][...])
    lower_ref[...] = total[:128] + dot_rows(arrow_ref[:6, :], factor)
    sent_ref[...] = lower_ref[ds(1 - core, 64), :]
    tail_ref[...] = jnp.zeros_like(tail_ref)
    tail_ref[:6, :] = total[128:134] + jnp.dot(
        tip_ref[...], factor, preferred_element_type=jnp.float32, precision=lax.Precision.HIGHEST
    )


def pick_columns(*refs):
    pieces, out = refs[:-1], refs[-1]
    _, z, _ = position()
    chunks = len(pieces) // SIDE
    blocks = 8 // chunks
    for piece in range(SIDE):
        rows = slice(128 * piece, 128 * piece + 128)
        for half in range(2):
            first = half * SIDE
            if blocks >= SIDE:
                source = pieces[(first // blocks) * SIDE + piece]
                value = source[:, ds(first % blocks + z, 128)]
            else:
                low = pieces[(first // blocks) * SIDE + piece][:, ds(lax.rem(z, blocks), 128)]
                high = pieces[(first // blocks + 1) * SIDE + piece][:, ds(lax.rem(z, blocks), 128)]
                value = jnp.where(z < blocks, low, high)
            out[rows, 128 * half : 128 * half + 128] = value


def turn_columns(own_ref, other_ref, high_ref, low_ref, all_ref):
    y, _, core = position()
    for half in range(2):
        columns = slice(128 * half, 128 * half + 128)
        all_ref[2 * core + half] = own_ref[:, columns].T
        all_ref[2 * (1 - core) + half] = other_ref[:, columns].T
    for distance in range(SIDE):
        rows = slice(128 * distance, 128 * distance + 128)
        high, low = split(all_ref[lax.rem(y + distance, SIDE)])
        high_ref[rows, :] = high
        low_ref[rows, :] = low


def sum_diagonal(*refs):
    parts, (factor_ref, tail_ref, kept_ref, sent_ref, all_ref, rows_ref) = refs[:4], refs[4:]
    y, z, core = position()
    factor = factor_rows(factor_ref, rows_ref, ds(y * SIDE + z, 128))
    total = (parts[0][...] + parts[1][...]) + (parts[2][...] + parts[3][...])
    all_ref[...] = total + dot_rows(factor, tail_ref[:6, :])
    kept_ref[...] = all_ref[ds(core, 64), :]
    sent_ref[...] = all_ref[ds(1 - core, 64), :]


def finish_lower(*refs):
    lowers, others = refs[:CHUNKS], refs[CHUNKS : 2 * CHUNKS]
    tails, other_tails = refs[2 * CHUNKS : 3 * CHUNKS], refs[3 * CHUNKS : 4 * CHUNKS]
    lower_ref, arrow_ref, tail_ref = refs[4 * CHUNKS :]
    y, z, core = position()
    width = lowers[0].shape[1]
    for chunk in range(CHUNKS):
        own = pl.ds(pl.multiple_of(core * 1024 + chunk * width, 128), width)
        other = pl.ds(pl.multiple_of((1 - core) * 1024 + chunk * width, 128), width)
        lower_ref[0, :, own] = -lowers[chunk][ds(core, 64), :]
        lower_ref[0, :, other] = -others[chunk][...]
        tail_ref[:, own] = tails[chunk][...]
        tail_ref[:, other] = other_tails[chunk][...]
    block = tail_ref[:, ds(y * SIDE + z, 128)]
    share = jnp.where(core == 0, block[:, :64], block[:, 64:])
    for row in range(6):
        arrow_ref[row] = -share[row : row + 1]


def sum_and_finish_lower(*refs):
    ins, outs, scratch = refs[: 6 + 4 * CHUNKS], refs[6 + 4 * CHUNKS : -3], refs[-3:]
    sum_diagonal(*ins[:6], *outs[:2], *scratch[:2])
    finish_lower(*ins[6:], *outs[2:], scratch[2])


def finish_diagonal(*refs):
    gram_ref, own_refs, other_refs, out_ref = refs[0], refs[1 : 1 + CHUNKS], refs[1 + CHUNKS : 1 + 2 * CHUNKS], refs[-1]
    _, _, core = position()
    width = own_refs[0].shape[1]
    for chunk in range(CHUNKS):
        own = pl.ds(pl.multiple_of(core * 1024 + chunk * width, 128), width)
        other = pl.ds(pl.multiple_of((1 - core) * 1024 + chunk * width, 128), width)
        out_ref[0, :, own] = gram_ref[0, :, own] + own_refs[chunk][...]
        out_ref[0, :, other] = gram_ref[0, :, other] + other_refs[chunk][...]


def per_device(separator_cov, separator_arrow, coupling, arrow_factor, arrow_tip, inverse_gram):
    width = 1024 // CHUNKS
    factor = arrow_factor.transpose(1, 0, 2)
    rows_scratch = [pltpu.VMEM((8, width), jnp.float32)]

    strips = call(
        cut_separator,
        [f32(72, 512)] + [f32(64, 512)] * 3,
        separator_cov[0],
        separator_arrow.transpose(1, 0, 2),
        name="cut_separator",
    )
    own_strips = [to_previous_step(strip, -distance) for distance, strip in enumerate(strips)]
    rows = coupling[0]
    starts = call(pair_rows, [f32(128, width)] * CHUNKS, rows, to_other_core(rows), name="pair_rows")

    def gathered(block):
        return [block] + [along_z(block, -distance) for distance in (1, 2, 3)]

    def scattered(shares):
        return [shares[0]] + [along_y(shares[distance], distance) for distance in (1, 2, 3)]

    pieces = [gathered(start) for start in starts]
    other_strips = [to_other_core(strip[:64]) for strip in own_strips]
    high, low, arrow = call(
        lay_separator, [bf16(528, 512), bf16(528, 512), f32(8, 128)], *own_strips, *other_strips, name="lay_separator"
    )

    lowers, sents, tails = [], [], []
    for chunk in range(CHUNKS):
        shares = call(multiply, [f32(136, width)] * SIDE, high, low, *pieces[chunk], name="multiply")
        lower, sent, tail = call(
            functools.partial(fold_lower, chunk),
            [f32(128, width), f32(64, width), f32(8, width)],
            *scattered(shares),
            arrow,
            factor,
            arrow_tip,
            name="fold_lower",
            scratch=rows_scratch,
        )
        lowers.append(lower)
        sents.append(sent)
        tails.append(tail)

    columns = call(pick_columns, f32(512, 256), *[piece for chunk in pieces for piece in chunk], name="pick_columns")
    turned = call(
        turn_columns,
        [bf16(512, 512)] * 2,
        columns,
        to_other_core(columns),
        name="turn_columns",
        scratch=[pltpu.VMEM((SIDE, 128, 512), jnp.float32)],
    )

    other_sents = [to_other_core(sent) for sent in sents]
    other_tails = [to_other_core(tail) for tail in tails]
    kept, others = [], []
    sum_scratch = [pltpu.VMEM((128, width), jnp.float32), pltpu.VMEM((8, 128), jnp.float32)]
    for chunk in range(CHUNKS):
        shares = call(multiply, [f32(128, width)] * SIDE, *turned, *gathered(lowers[chunk]), name="multiply")
        operands = [*scattered(shares), factor, tails[chunk]]
        if chunk == CHUNKS - 2:
            mine, sent, lower_out, arrow_out = call(
                sum_and_finish_lower,
                [f32(64, width), f32(64, width), given(1, 64, 2048), given(6, 1, 64)],
                *operands,
                *lowers,
                *other_sents,
                *tails,
                *other_tails,
                name="sum_and_finish_lower",
                scratch=[*sum_scratch, pltpu.VMEM((8, 2048), jnp.float32)],
            )
        else:
            mine, sent = call(
                sum_diagonal, [f32(64, width)] * 2, *operands, name="sum_diagonal", scratch=sum_scratch
            )
        kept.append(mine)
        others.append(to_other_core(sent))
    diag_out = call(finish_diagonal, given(1, 64, 2048), inverse_gram, *kept, *others, name="finish_diagonal")
    return diag_out, lower_out, arrow_out.transpose(1, 0, 2)


def solution(mesh):
    return jax.shard_map(
        per_device,
        mesh=mesh,
        in_specs=(
            P("tm", "panel", None),
            P("tm", None, None),
            P("tm", "panel", None),
            P("tm", None, None),
            P(),
            P("tm", "panel", None),
        ),
        out_specs=(P("tm", "panel", None), P("tm", "panel", None), P("tm", None, "panel")),
        check_vma=False,
    )
```

```python
import functools

import jax
import jax.numpy as jnp
from jax import lax
from jax.experimental import pallas as pl
from jax.experimental.pallas import tpu as pltpu
from jax.sharding import PartitionSpec as P

SIDE = 4
CHUNKS = 2
GRANT = 12 * 2**20


def panel_index(y, z, core):
    return (y % SIDE) * 2 * SIDE + (z % SIDE) * 2 + core


def route(target):
    places = [(y, z, core) for y in range(SIDE) for z in range(SIDE) for core in range(2)]
    return [(panel_index(*place), panel_index(*target(*place))) for place in places]


def turned_place(place, over, along):
    y, z, core = place
    return (y + over, z + along, core) if core == 0 else (y + along, z + over, core)


def across(block, distance):
    return lax.ppermute(block, "panel", route(lambda *place: turned_place(place, distance, 0)))


def in_line(block, distance):
    return lax.ppermute(block, "panel", route(lambda *place: turned_place(place, 0, distance)))


def to_other_core(block):
    return lax.ppermute(block, "panel", route(lambda y, z, core: (y, z, 1 - core)))


def to_previous_step(block):
    size = lax.axis_size("tm")
    return lax.ppermute(block, "tm", [(step, step - 1) for step in range(1, size)])


def position():
    index = lax.axis_index("panel")
    return index // (2 * SIDE), (index // 2) % SIDE, index % 2


def line_position():
    y, z, core = position()
    return jnp.where(core == 0, y, z), jnp.where(core == 0, z, y)


def chip_block(line, place):
    _, _, core = position()
    line, place = lax.rem(line, SIDE), lax.rem(place, SIDE)
    return jnp.where(core == 0, line * SIDE + place, place * SIDE + line)


def ds(index, size):
    return pl.ds(pl.multiple_of(index * size, size), size)


def split(value):
    high = value.astype(jnp.bfloat16)
    return high, (value - high.astype(jnp.float32)).astype(jnp.bfloat16)


def dot(left, right):
    return jnp.dot(left, right, preferred_element_type=jnp.float32)


def dot_rows(left, right):
    return lax.dot_general(
        left, right, (((0,), (0,)), ((), ())), preferred_element_type=jnp.float32, precision=lax.Precision.HIGHEST
    )


def call(kernel, out_shape, *operands, name, scratch=()):
    spec = pl.BlockSpec(memory_space=pltpu.VMEM)
    return pl.pallas_call(
        kernel,
        out_shape=out_shape,
        in_specs=[spec] * len(operands),
        out_specs=jax.tree.map(lambda _: spec, out_shape),
        scratch_shapes=scratch,
        compiler_params=pltpu.CompilerParams(vmem_limit_bytes=GRANT),
        name=name,
    )(*[pltpu.with_memory_space_constraint(operand, pltpu.VMEM) for operand in operands])


def f32(*shape):
    return pltpu.VMEM(shape, jnp.float32)


def bf16(*shape):
    return pltpu.VMEM(shape, jnp.bfloat16)


def given(*shape):
    return jax.ShapeDtypeStruct(shape, jnp.float32)


def cut_separator(own_ref, other_ref, *out_refs):
    _, _, core = position()
    line, place = line_position()
    for distance, out in enumerate(out_refs):
        for block in range(SIDE):
            columns = ds(chip_block(line + SIDE - distance, place + block), 128)
            to = slice(128 * block, 128 * block + 128)
            out[ds(core, 64), to] = own_ref[:, columns]
            out[ds(1 - core, 64), to] = other_ref[:, columns]


def pair_rows(own_ref, other_ref, *out_refs):
    _, _, core = position()
    line, place = line_position()
    half = ds(core, 1024)
    for distance, out in enumerate(out_refs):
        for where, source in ((core, own_ref), (1 - core, other_ref)):
            rows = ds(where, 64)
            out[rows, :1024] = source[:, half]
            for strip in range(SIDE):
                columns = ds(chip_block(line + strip, place + SIDE - distance), 128)
                out[rows, 1024 + 128 * strip : 1152 + 128 * strip] = source[:, columns]


def lay_separator(*refs):
    pieces, (arrow_ref, high_ref, low_ref, rows_ref) = refs[:4], refs[4:]
    line, place = line_position()
    for distance in range(SIDE):
        rows = slice(128 * distance, 128 * distance + 128)
        high_ref[rows, :], low_ref[rows, :] = split(pieces[distance][...])
    rows_ref[...] = jnp.zeros_like(rows_ref)
    for block in range(SIDE):
        columns = ds(chip_block(line, place + block), 128)
        for row in range(6):
            rows_ref[row : row + 1, 128 * block : 128 * block + 128] = arrow_ref[row, :, columns]
    high_ref[512:, :], low_ref[512:, :] = split(rows_ref[...])


def multiply(chunk, *refs):
    (high_ref, low_ref), pieces, outs = refs[:2], refs[2:6], refs[6:]
    width = outs[0].shape[1]
    columns = slice(chunk * width, chunk * width + width)
    high, low = split(jnp.concatenate([piece[:, columns] for piece in pieces]))
    left_high, left_low = high_ref[...], low_ref[...]
    product = dot(left_high, high) + (dot(left_high, low) + dot(left_low, high))
    for distance, out in enumerate(outs):
        out[:128, :] = product[128 * distance : 128 * distance + 128]
        if out.shape[0] > 128:
            out[128:, :] = product[512:520]


def factor_rows(factor_ref, rows_ref, columns):
    for row in range(6):
        rows_ref[row : row + 1, :] = factor_ref[row, :, columns]
    return rows_ref[:6, :]


def fold_lower(chunk, *refs):
    parts, (arrow_ref, factor_ref, tip_ref, lower_ref, sent_ref, tail_ref, rows_ref, arrow_rows_ref) = refs[:4], refs[4:]
    y, z, core = position()
    width = lower_ref.shape[1]
    factor = factor_rows(factor_ref, rows_ref, pl.ds(pl.multiple_of(core * 1024 + chunk * width, 128), width))
    arrow = factor_rows(arrow_ref, arrow_rows_ref, ds(y * SIDE + z, 128))
    total = (parts[0][...] + parts[1][...]) + (parts[2][...] + parts[3][...])
    lower_ref[...] = total[:128] + dot_rows(arrow, factor)
    sent_ref[...] = lower_ref[ds(1 - core, 64), :]
    tail_ref[...] = jnp.zeros_like(tail_ref)
    tail_ref[:6, :] = total[128:134] + jnp.dot(
        tip_ref[...], factor, preferred_element_type=jnp.float32, precision=lax.Precision.HIGHEST
    )


def turn_strips(*refs):
    pieces, (high_ref, low_ref) = refs[:4], refs[4:]
    for strip in range(SIDE):
        rows = slice(128 * strip, 128 * strip + 128)
        for place, piece in enumerate(pieces):
            columns = slice(128 * place, 128 * place + 128)
            high_ref[rows, columns], low_ref[rows, columns] = split(piece[:, 1024 + 128 * strip : 1152 + 128 * strip].T)


def sum_diagonal(*refs):
    parts, (factor_ref, tail_ref, kept_ref, sent_ref, all_ref, rows_ref) = refs[:4], refs[4:]
    y, z, core = position()
    factor = factor_rows(factor_ref, rows_ref, ds(y * SIDE + z, 128))
    total = (parts[0][...] + parts[1][...]) + (parts[2][...] + parts[3][...])
    all_ref[...] = total + dot_rows(factor, tail_ref[:6, :])
    kept_ref[...] = all_ref[ds(core, 64), :]
    sent_ref[...] = all_ref[ds(1 - core, 64), :]


def finish_lower(*refs):
    lowers, others = refs[:CHUNKS], refs[CHUNKS : 2 * CHUNKS]
    tails, other_tails = refs[2 * CHUNKS : 3 * CHUNKS], refs[3 * CHUNKS : 4 * CHUNKS]
    lower_ref, arrow_ref, tail_ref = refs[4 * CHUNKS :]
    y, z, core = position()
    width = lowers[0].shape[1]
    for chunk in range(CHUNKS):
        own = pl.ds(pl.multiple_of(core * 1024 + chunk * width, 128), width)
        other = pl.ds(pl.multiple_of((1 - core) * 1024 + chunk * width, 128), width)
        lower_ref[0, :, own] = -lowers[chunk][ds(core, 64), :]
        lower_ref[0, :, other] = -others[chunk][...]
        tail_ref[:, own] = tails[chunk][...]
        tail_ref[:, other] = other_tails[chunk][...]
    block = tail_ref[:, ds(y * SIDE + z, 128)]
    share = jnp.where(core == 0, block[:, :64], block[:, 64:])
    for row in range(6):
        arrow_ref[row] = -share[row : row + 1]


def sum_and_finish_lower(*refs):
    ins, outs, scratch = refs[: 6 + 4 * CHUNKS], refs[6 + 4 * CHUNKS : -3], refs[-3:]
    sum_diagonal(*ins[:6], *outs[:2], *scratch[:2])
    finish_lower(*ins[6:], *outs[2:], scratch[2])


def finish_diagonal(*refs):
    gram_ref, own_refs, other_refs, out_ref = refs[0], refs[1 : 1 + CHUNKS], refs[1 + CHUNKS : 1 + 2 * CHUNKS], refs[-1]
    _, _, core = position()
    width = own_refs[0].shape[1]
    for chunk in range(CHUNKS):
        own = pl.ds(pl.multiple_of(core * 1024 + chunk * width, 128), width)
        other = pl.ds(pl.multiple_of((1 - core) * 1024 + chunk * width, 128), width)
        out_ref[0, :, own] = gram_ref[0, :, own] + own_refs[chunk][...]
        out_ref[0, :, other] = gram_ref[0, :, other] + other_refs[chunk][...]


def per_device(separator_cov, separator_arrow, coupling, arrow_factor, arrow_tip, inverse_gram):
    width = 1024 // CHUNKS
    factor = arrow_factor.transpose(1, 0, 2)
    fold_scratch = [pltpu.VMEM((8, width), jnp.float32), pltpu.VMEM((8, 128), jnp.float32)]

    next_cov = to_previous_step(separator_cov[0])
    arrow = to_previous_step(separator_arrow.transpose(1, 0, 2))
    rows = coupling[0]
    sent_rows = call(pair_rows, [f32(128, 1536)] * SIDE, rows, to_other_core(rows), name="pair_rows")

    def spread(blocks, move, sign):
        moved = {distance: move(blocks[distance], sign * distance) for distance in (1, 3, 2)}
        return [blocks[0], moved[1], moved[2], moved[3]]

    pieces = spread(sent_rows, in_line, -1)
    cuts = call(cut_separator, [f32(128, 512)] * SIDE, next_cov, to_other_core(next_cov), name="cut_separator")
    high, low = call(
        lay_separator,
        [bf16(520, 512)] * 2,
        *spread(cuts, across, -1),
        arrow,
        name="lay_separator",
        scratch=[pltpu.VMEM((8, 512), jnp.float32)],
    )

    lowers, sents, tails = [], [], []
    for chunk in range(CHUNKS):
        shares = call(
            functools.partial(multiply, chunk), [f32(136, width)] * SIDE, high, low, *pieces, name="multiply"
        )
        lower, sent, tail = call(
            functools.partial(fold_lower, chunk),
            [f32(128, width), f32(64, width), f32(8, width)],
            *spread(shares, across, 1),
            arrow,
            factor,
            arrow_tip,
            name="fold_lower",
            scratch=fold_scratch,
        )
        lowers.append(lower)
        sents.append(sent)
        tails.append(tail)

    turned = call(turn_strips, [bf16(512, 512)] * 2, *pieces, name="turn_strips")

    other_sents = [to_other_core(sent) for sent in sents]
    other_tails = [to_other_core(tail) for tail in tails]
    kept, others = [], []
    sum_scratch = [pltpu.VMEM((128, width), jnp.float32), pltpu.VMEM((8, 128), jnp.float32)]
    for chunk in range(CHUNKS):
        lines = spread([lowers[chunk]] * SIDE, in_line, -1)
        shares = call(functools.partial(multiply, 0), [f32(128, width)] * SIDE, *turned, *lines, name="multiply")
        operands = [*spread(shares, across, 1), factor, tails[chunk]]
        if chunk == CHUNKS - 2:
            mine, sent, lower_out, arrow_out = call(
                sum_and_finish_lower,
                [f32(64, width), f32(64, width), given(1, 64, 2048), given(6, 1, 64)],
                *operands,
                *lowers,
                *other_sents,
                *tails,
                *other_tails,
                name="sum_and_finish_lower",
                scratch=[*sum_scratch, pltpu.VMEM((8, 2048), jnp.float32)],
            )
        else:
            mine, sent = call(
                sum_diagonal, [f32(64, width)] * 2, *operands, name="sum_diagonal", scratch=sum_scratch
            )
        kept.append(mine)
        others.append(to_other_core(sent))
    diag_out = call(finish_diagonal, given(1, 64, 2048), inverse_gram, *kept, *others, name="finish_diagonal")
    return diag_out, lower_out, arrow_out.transpose(1, 0, 2)


def solution(mesh):
    return jax.shard_map(
        per_device,
        mesh=mesh,
        in_specs=(
            P("tm", "panel", None),
            P("tm", None, None),
            P("tm", "panel", None),
            P("tm", None, None),
            P(),
            P("tm", "panel", None),
        ),
        out_specs=(P("tm", "panel", None), P("tm", "panel", None), P("tm", None, "panel")),
        check_vma=False,
    )
```
